32 devices in a mesh: dp: 4 (over z), section: 2 (over core), bfly: 4 (over y, x).
Axes of the slice: x: 2, y: 2, z: 4, core: 2. Of those that a mesh axis runs over, the one named last changes fastest.
Arguments:
- activations: bfloat16 [3, 1024, 8192], P(None, 'dp', 'bfly'), may hold values from -6 to 6
- cotangent: bfloat16 [3, 1024, 8192], P(None, 'dp', 'bfly'), may hold values from -0.25 to 0.25
- up_left: bfloat16 [2, 64, 128, 128], P('section', 'bfly'), may hold values from -0.5 to 0.5
- up_right: bfloat16 [2, 128, 64, 256], P('section', 'bfly'), may hold values from -0.75 to 0.75
- down_left: bfloat16 [2, 128, 64, 256], P('section', 'bfly'), may hold values from -0.375 to 0.375
- down_right: bfloat16 [2, 64, 128, 128], P('section', 'bfly'), may hold values from -0.5 to 0.5
Outputs:
- grad_up_left: float32 [2, 64, 128, 128], P('section', 'bfly')
- grad_up_right: float32 [2, 128, 64, 256], P('section', 'bfly')
- grad_down_left: float32 [2, 128, 64, 256], P('section', 'bfly')
- grad_down_right: float32 [2, 64, 128, 128], P('section', 'bfly')
The draws below stay inside these ranges and needn't reach their ends.
All inputs are finite; a program needn't handle non-finite values.
Results may differ from the reference program's by a relative error of at most 0.011.
Values may be sent and summed in bfloat16 or wider, within the bound.
A program may use at most 128 MiB of HBM per device.

```python
import jax
import jax.numpy as jnp

NB = 64
BS = 128
HB = 256
D = 8192
MB = 3
ROWS = 1024
LAYERS = 2


def shard_levels(key, extent, shards, least, largest):
    def one(dim, parts):
        heights = jax.random.uniform(jax.random.fold_in(jax.random.fold_in(key, 6), dim), (parts,), jnp.float32, least / len(shards), largest / len(shards))
        return jnp.repeat(jnp.exp(heights), extent[dim] // parts).reshape((-1,) + (1,) * (len(extent) - dim - 1))

    factor_of = one(*shards[0])
    for cut in shards[1:]:
        factor_of = factor_of * one(*cut)
    return factor_of


def noise(rng, extent, width, most, split=(), held_as=jnp.bfloat16):
    drawn = jax.random.normal(rng, extent, jnp.float32) * width
    if len(split) > 0:
        drawn = shard_levels(rng, extent, split, -0.22, 0.18) * drawn
    return jnp.clip(drawn, min=-most, max=most).astype(held_as)


def setup_inputs(seed: int = 0) -> dict:
    arg_keys = jax.random.split(jax.random.key(seed), 7)
    activations = noise(arg_keys[0], (MB, ROWS, D), 1.0, 6.0, ((1, 4), (2, 4)))
    cotangent = noise(arg_keys[1], (MB, ROWS, D), (1.0 / (MB * ROWS) ** 0.5), 0.25, ((1, 4), (2, 4)))
    up_left = noise(arg_keys[2], (LAYERS, NB, BS, BS), BS ** -0.5, 0.5, ((0, 2), (1, 4)))
    up_right = noise(arg_keys[3], (LAYERS, BS, NB, HB), NB ** -0.5, 0.75, ((0, 2), (1, 4)))
    down_left = noise(arg_keys[4], (LAYERS, BS, NB, HB), HB ** -0.5, 0.375, ((0, 2), (1, 4)))
    down_right = noise(arg_keys[5], (LAYERS, NB, BS, BS), BS ** -0.5, 0.5, ((0, 2), (1, 4)))
    return dict(activations=activations, cotangent=cotangent, up_left=up_left, up_right=up_right, down_left=down_left, down_right=down_right)


def slope_of(hidden):
    sigmoid = jax.nn.sigmoid(hidden)
    return sigmoid * (1.0 + hidden * (1.0 - sigmoid))


def expand_up(layer_in, left_up, right_up, left_down):
    lowered = jnp.einsum('rai,aij->raj', layer_in.astype(jnp.float32), left_up.astype(jnp.float32)).astype(jnp.bfloat16)
    hidden = jnp.einsum('raj,jaq->rjq', lowered.astype(jnp.float32), right_up.astype(jnp.float32))
    gated = jax.nn.silu(hidden).astype(jnp.bfloat16)
    mixed = jnp.einsum('rjq,jaq->rja', gated.astype(jnp.float32), left_down.astype(jnp.float32)).astype(jnp.bfloat16)
    return lowered, hidden, gated, mixed


def reference(activations, cotangent, up_left, up_right, down_left, down_right):
    total_rows = MB * ROWS
    layer_in = activations.reshape(total_rows, NB, BS)
    inputs_kept = []
    for layer in range(LAYERS):
        inputs_kept.append(layer_in)
        unused_a, unused_b, unused_c, mixed = expand_up(layer_in, up_left[layer], up_right[layer], down_left[layer])
        branch = jnp.einsum('rja,aji->rai', mixed.astype(jnp.float32), down_right[layer].astype(jnp.float32))
        layer_in = (layer_in.astype(jnp.float32) + branch).astype(jnp.bfloat16)
    upstream = cotangent.reshape(total_rows, NB, BS)
    grads_ul = []
    grads_ur = []
    grads_dl = []
    grads_dr = []
    for layer in range(LAYERS - 1, -1, -1):
        saved = inputs_kept[layer]
        lowered, hidden, gated, mixed = expand_up(saved, up_left[layer], up_right[layer], down_left[layer])
        upstream32 = upstream.astype(jnp.float32)
        grads_dr.append(jnp.einsum('rja,rai->aji', mixed.astype(jnp.float32), upstream32))
        mixed_grad = jnp.einsum('rai,aji->rja', upstream32, down_right[layer].astype(jnp.float32)).astype(jnp.bfloat16)
        grads_dl.append(jnp.einsum('rjq,rja->jaq', gated.astype(jnp.float32), mixed_grad.astype(jnp.float32)))
        gated_grad = jnp.einsum('rja,jaq->rjq', mixed_grad.astype(jnp.float32), down_left[layer].astype(jnp.float32))
        hidden_grad = (gated_grad * slope_of(hidden)).astype(jnp.bfloat16)
        grads_ur.append(jnp.einsum('raj,rjq->jaq', lowered.astype(jnp.float32), hidden_grad.astype(jnp.float32)))
        lowered_grad = jnp.einsum('rjq,jaq->raj', hidden_grad.astype(jnp.float32), up_right[layer].astype(jnp.float32)).astype(jnp.bfloat16)
        grads_ul.append(jnp.einsum('rai,raj->aij', saved.astype(jnp.float32), lowered_grad.astype(jnp.float32)))
        upstream = (upstream32 + jnp.einsum('raj,aij->rai', lowered_grad.astype(jnp.float32), up_left[layer].astype(jnp.float32))).astype(jnp.bfloat16)
    grad_up_left = jnp.stack(grads_ul[::-1])
    grad_up_right = jnp.stack(grads_ur[::-1])
    grad_down_left = jnp.stack(grads_dl[::-1])
    grad_down_right = jnp.stack(grads_dr[::-1])
    return (grad_up_left, grad_up_right, grad_down_left, grad_down_right)
```

```python
import jax
import jax.numpy as jnp
from jax import lax
from jax.sharding import PartitionSpec as P

CHUNKS = 1
BF = jnp.bfloat16
F32 = jnp.float32


def dot(spec, x, y):
    return jnp.einsum(spec, x, y, preferred_element_type=F32)


def to_hidden(block):
    return lax.all_to_all(block, "bfly", split_axis=0, concat_axis=1, tiled=True)


def to_feature(block):
    return lax.all_to_all(block, "bfly", split_axis=1, concat_axis=0, tiled=True)


def both_layers(own):
    segments = lax.axis_size("section")
    place = lax.axis_index("section")
    if segments == 1:
        return [own[layer] for layer in range(own.shape[0])]
    other = lax.ppermute(own[0], "section", [(0, 1), (1, 0)])
    return [jnp.where(place == 0, own[0], other), jnp.where(place == 0, other, own[0])]


def reduce_layer(grad):
    place = lax.axis_index("section")
    half = grad.shape[0] // 2
    grad16 = grad.astype(BF)
    theirs = lax.dynamic_slice_in_dim(grad16, (1 - place) * half, half, 0)
    mine = lax.dynamic_slice_in_dim(grad, place * half, half, 0)
    got = lax.ppermute(theirs, "section", [(0, 1), (1, 0)])
    part = (mine + got.astype(F32)).astype(BF)
    return lax.psum(part, "dp")


def on_device(activations, cotangent, up_left, up_right, down_left, down_right):
    place = lax.axis_index("section")
    segments = lax.axis_size("section")
    micro, row_count, cols = activations.shape
    rows = row_count // segments
    blocks, width = up_left.shape[1], up_left.shape[2]
    A = both_layers(up_left)
    B = both_layers(up_right)
    C = both_layers(down_left)
    E = both_layers(down_right)

    def columns(whole):
        part = lax.dynamic_slice_in_dim(whole, place * rows, rows, 1)
        part = part.reshape(CHUNKS, micro * rows // CHUNKS, blocks, width)
        return [jnp.transpose(part[c], (1, 2, 0)) for c in range(CHUNKS)]

    x = columns(activations)
    y = columns(cotangent)
    kept = []
    for layer in range(2):
        u = [to_feature(dot("ait,aij->ajt", b, A[layer]).astype(BF)) for b in x]
        h = [dot("ajt,jaq->jqt", b, B[layer]) for b in u]
        g = [jax.nn.silu(b).astype(BF) for b in h]
        w = [to_feature(dot("jqt,jaq->jat", b, C[layer]).astype(BF)) for b in g]
        kept.append((x, u, h, g, w))
        if layer == 0:
            x = [
                (b.astype(F32) + dot("jat,aji->ait", m, E[layer])).astype(BF)
                for b, m in zip(x, w)
            ]
    outs = [None, None]
    for layer in (1, 0):
        x, u, h, g, w = kept[layer]
        dw = [to_hidden(dot("ait,aji->jat", b, E[layer]).astype(BF)) for b in y]
        g_dr = sum(dot("jat,ait->aji", p, q) for p, q in zip(w, y))
        g_dl = sum(dot("jqt,jat->jaq", p, q) for p, q in zip(g, dw))
        dh = []
        for p, q in zip(dw, h):
            s = jax.nn.sigmoid(q)
            dg = dot("jat,jaq->jqt", p, C[layer])
            dh.append((dg * (s * (1.0 + q * (1.0 - s)))).astype(BF))
        du = [to_hidden(dot("jqt,jaq->ajt", b, B[layer]).astype(BF)) for b in dh]
        g_ur = sum(dot("ajt,jqt->jaq", p, q) for p, q in zip(u, dh))
        g_ul = sum(dot("ait,ajt->aij", p, q) for p, q in zip(x, du))
        if layer == 1:
            y = [
                (b.astype(F32) + dot("ajt,aij->ait", p, A[layer])).astype(BF)
                for b, p in zip(y, du)
            ]
        outs[layer] = [reduce_layer(v) for v in (g_ul, g_ur, g_dl, g_dr)]
    final = []
    for first, second in zip(outs[0], outs[1]):
        send = jnp.where(place == 0, second, first)
        keep = jnp.where(place == 0, first, second)
        got = lax.ppermute(send, "section", [(0, 1), (1, 0)])
        low = jnp.where(place == 0, keep, got)
        high = jnp.where(place == 0, got, keep)
        final.append(jnp.concatenate([low, high], 0).astype(F32)[None])
    return tuple(final)


def solution(mesh):
    weight = P("section", "bfly", None, None)
    token = P(None, "dp", "bfly")
    return jax.shard_map(
        on_device,
        mesh=mesh,
        in_specs=(token, token, weight, weight, weight, weight),
        out_specs=(weight, weight, weight, weight),
        check_vma=False,
    )
```

```python
import functools

import jax
import jax.numpy as jnp
from jax import lax
from jax.experimental import pallas as pl
from jax.experimental.pallas import tpu as pltpu
from jax.sharding import PartitionSpec as P

CHUNKS = 1
GROUPS = (
    (("dl", 1), ("ur", 1), ("dr", 1)),
    (("dl", 0), ("ur", 0)),
)
LINE = (("dr", 0), ("ul", 1), ("ul", 0))
BF = jnp.bfloat16
F32 = jnp.float32
MESH = pl.DeviceIdType.MESH


def dot(spec, x, y):
    return jnp.einsum(spec, x, y, preferred_element_type=F32)


def to_hidden(block):
    return lax.all_to_all(block, "bfly", split_axis=0, concat_axis=1, tiled=True)


def to_feature(block):
    return lax.all_to_all(block, "bfly", split_axis=1, concat_axis=0, tiled=True)


def both_layers(own):
    segments = lax.axis_size("section")
    place = lax.axis_index("section")
    if segments == 1:
        return [own[layer] for layer in range(own.shape[0])]
    other = lax.ppermute(own[0], "section", [(0, 1), (1, 0)])
    return [jnp.where(place == 0, own[0], other), jnp.where(place == 0, other, own[0])]


def pair_sum(grad):
    place = lax.axis_index("section")
    half = grad.shape[0] // 2
    theirs = lax.dynamic_slice_in_dim(grad, (1 - place) * half, half, 0).astype(BF)
    mine = lax.dynamic_slice_in_dim(grad, place * half, half, 0)
    got = lax.ppermute(theirs, "section", [(0, 1), (1, 0)])
    return (mine + got.astype(F32)).astype(BF)


def summed(parts, before):
    if before is not None:
        parts, before = lax.optimization_barrier((parts, before))
    return lax.psum(parts, "dp"), before


def line_sum_kernel(n, count, *refs):
    x, o, rr, rl, sr, sl = (refs[k * count : (k + 1) * count] for k in range(6))
    sent, landed = refs[6 * count :]
    me = lax.axis_index("dp")
    has_left, has_right = me > 0, me < n - 1
    barrier = pltpu.get_barrier_semaphore()

    @pl.when(has_left)
    def _():
        pl.semaphore_signal(barrier, inc=1, device_id={"dp": me - 1}, device_id_type=MESH)

    @pl.when(has_right)
    def _():
        pl.semaphore_signal(barrier, inc=1, device_id={"dp": me + 1}, device_id_type=MESH)

    @pl.when(has_left & has_right)
    def _():
        pl.semaphore_wait(barrier, 2)

    @pl.when((me == 0) | (me == n - 1))
    def _():
        pl.semaphore_wait(barrier, 1)

    def rows(leaf, c):
        depth = x[leaf].shape[0] // n
        return pl.ds(pl.multiple_of(c * depth, depth), depth)

    def copy(leaf, kind, c, src, dst):
        part = rows(leaf, c)
        target = lax.rem(me + 1, n) if kind % 2 == 0 else lax.rem(me + n - 1, n)
        return pltpu.make_async_remote_copy(
            src_ref=src[leaf].at[part],
            dst_ref=dst[leaf].at[part],
            send_sem=sent.at[leaf, kind, c],
            recv_sem=landed.at[leaf, kind, c],
            device_id={"dp": target},
            device_id_type=MESH,
        )

    def running(leaf, c, got, out):
        part = rows(leaf, c)
        total = x[leaf][part, :].astype(F32) + got[leaf][part, :].astype(F32)
        out[leaf][part, :] = total.astype(BF)

    for leaf in range(count):
        for step in range(n - 1):

            @pl.when(me == 0)
            def _():
                copy(leaf, 0, n - 1 - step, x, rr).start()

            @pl.when(me == n - 1)
            def _():
                copy(leaf, 1, step, x, rl).start()

    for leaf in range(count):
        for step in range(n - 1):
            c = n - 1 - step

            @pl.when(has_left & (me <= c))
            def _():
                copy(leaf, 0, c, sr, rr).wait_recv()

            @pl.when(has_left & (me < c))
            def _():
                running(leaf, c, rr, sr)
                copy(leaf, 0, c, sr, rr).start()

            d = step

            @pl.when(has_right & (me >= d))
            def _():
                copy(leaf, 1, d, sl, rl).wait_recv()

            @pl.when(has_right & (me > d))
            def _():
                running(leaf, d, rl, sl)
                copy(leaf, 1, d, sl, rl).start()

        @pl.when(has_left & has_right)
        def _():
            part = rows(leaf, me)
            total = x[leaf][part, :].astype(F32) + rr[leaf][part, :].astype(F32)
            o[leaf][part, :] = (total + rl[leaf][part, :].astype(F32)).astype(BF)

        @pl.when(me == 0)
        def _():
            running(leaf, 0, rl, o)

        @pl.when(me == n - 1)
        def _():
            running(leaf, n - 1, rr, o)

        @pl.when(has_right)
        def _():
            copy(leaf, 2, me, o, o).start()

        @pl.when(has_left)
        def _():
            copy(leaf, 3, me, o, o).start()

    for leaf in range(count):
        for far in range(1, n):

            @pl.when(me - far >= 0)
            def _():
                copy(leaf, 2, me - far, o, o).wait_recv()

            @pl.when((me - far >= 0) & has_right)
            def _():
                copy(leaf, 2, me - far, o, o).start()

            @pl.when(me + far <= n - 1)
            def _():
                copy(leaf, 3, me + far, o, o).wait_recv()

            @pl.when((me + far <= n - 1) & has_left)
            def _():
                copy(leaf, 3, me + far, o, o).start()

    for leaf in range(count):
        for c in range(n):

            @pl.when(me < c)
            def _():
                copy(leaf, 0, c, sr, rr).wait_send()

            @pl.when(me > c)
            def _():
                copy(leaf, 1, c, sl, rl).wait_send()

            @pl.when((c <= me) & has_right)
            def _():
                copy(leaf, 2, c, o, o).wait_send()

            @pl.when((c >= me) & has_left)
            def _():
                copy(leaf, 3, c, o, o).wait_send()


def line_sum(parts):
    n = lax.axis_size("dp")
    flat = [p.reshape(-1, p.shape[-1]) for p in parts]
    count = len(flat)
    size = sum(p.size for p in flat)
    shapes = [jax.ShapeDtypeStruct(p.shape, BF) for p in flat]
    got = pl.pallas_call(
        functools.partial(line_sum_kernel, n, count),
        out_shape=shapes,
        in_specs=[pl.BlockSpec(memory_space=pltpu.VMEM)] * count,
        out_specs=[pl.BlockSpec(memory_space=pltpu.VMEM)] * count,
        scratch_shapes=[pltpu.VMEM(p.shape, BF) for p in flat] * 4
        + [pltpu.SemaphoreType.DMA((count, 4, n)), pltpu.SemaphoreType.DMA((count, 4, n))],
        compiler_params=pltpu.CompilerParams(collective_id=0, has_side_effects=True),
        cost_estimate=pl.CostEstimate(flops=0, bytes_accessed=size * 2 * 60, transcendentals=0),
        name="line_sum",
    )(*flat)
    return [g.reshape(p.shape) for g, p in zip(got, parts)]


def on_device(activations, cotangent, up_left, up_right, down_left, down_right):
    place = lax.axis_index("section")
    segments = lax.axis_size("section")
    micro, row_count, cols = activations.shape
    rows = row_count // segments
    blocks, width = up_left.shape[1], up_left.shape[2]
    A = both_layers(up_left)
    B = both_layers(up_right)
    C = both_layers(down_left)
    E = both_layers(down_right)

    def columns(whole):
        part = lax.dynamic_slice_in_dim(whole, place * rows, rows, 1)
        part = part.reshape(CHUNKS, micro * rows // CHUNKS, blocks, width)
        return [jnp.transpose(part[c], (1, 2, 0)) for c in range(CHUNKS)]

    x = columns(activations)
    y = columns(cotangent)
    kept = []
    for layer in range(2):
        u = [to_feature(dot("ait,aij->ajt", b, A[layer]).astype(BF)) for b in x]
        g, slope = [], []
        for b in u:
            h = dot("ajt,jaq->jqt", b, B[layer])
            s = jax.nn.sigmoid(h)
            g.append((h * s).astype(BF))
            slope.append((s * (1.0 + h * (1.0 - s))).astype(BF))
        w = [to_feature(dot("jqt,jaq->jat", b, C[layer]).astype(BF)) for b in g]
        kept.append((x, u, slope, g, w))
        if layer == 0:
            x = [
                (b.astype(F32) + dot("jat,aji->ait", m, E[layer])).astype(BF)
                for b, m in zip(x, w)
            ]
    sums = {}
    for layer in (1, 0):
        x, u, slope, g, w = kept[layer]
        dw = [to_hidden(dot("ait,aji->jat", b, E[layer]).astype(BF)) for b in y]
        dh = [
            (dot("jat,jaq->jqt", p, C[layer]) * q.astype(F32)).astype(BF)
            for p, q in zip(dw, slope)
        ]
        du = [to_hidden(dot("jqt,jaq->ajt", b, B[layer]).astype(BF)) for b in dh]
        sums["dr", layer] = pair_sum(sum(dot("jat,ait->aji", p, q) for p, q in zip(w, y)))
        sums["dl", layer] = pair_sum(sum(dot("jqt,jat->jaq", p, q) for p, q in zip(g, dw)))
        sums["ur", layer] = pair_sum(sum(dot("ajt,jqt->jaq", p, q) for p, q in zip(u, dh)))
        sums["ul", layer] = pair_sum(sum(dot("ait,ajt->aij", p, q) for p, q in zip(x, du)))
        if layer == 1:
            y = [
                (b.astype(F32) + dot("ajt,aij->ait", p, A[layer])).astype(BF)
                for b, p in zip(y, du)
            ]
    last, before = (), None
    for group in GROUPS + ((),):
        if group:
            got, before = summed([sums[key] for key in group], before)
        for key, value in zip(last, before or ()):
            sums[key] = value
        last, before = group, got
    for key, value in zip(LINE, line_sum([sums[key] for key in LINE])):
        sums[key] = value
    outs = [[sums[name, layer] for name in ("ul", "ur", "dl", "dr")] for layer in range(2)]
    final = []
    for first, second in zip(outs[0], outs[1]):
        send = jnp.where(place == 0, second, first)
        keep = jnp.where(place == 0, first, second)
        got = lax.ppermute(send, "section", [(0, 1), (1, 0)])
        low = jnp.where(place == 0, keep, got)
        high = jnp.where(place == 0, got, keep)
        final.append(jnp.concatenate([low, high], 0).astype(F32)[None])
    return tuple(final)


def solution(mesh):
    weight = P("section", "bfly", None, None)
    token = P(None, "dp", "bfly")
    return jax.shard_map(
        on_device,
        mesh=mesh,
        in_specs=(token, token, weight, weight, weight, weight),
        out_specs=(weight, weight, weight, weight),
        check_vma=False,
    )
```
